32 devices in a mesh: dp: 8 (over z, x), fsdp: 4 (over y, core).
Axes of the slice: x: 2, y: 2, z: 4, core: 2. Of those that a mesh axis runs over, the one named last changes fastest.
Arguments:
- tokens: bfloat16 [8192, 1024], P(('dp', 'fsdp'))
- segments: int32 [64, 128], P(('dp', 'fsdp')), may hold values from 0 to 7, never falling along the last dimension, each value on 1 to 64 neighbouring positions
- w_qkv: bfloat16 [1024, 3072], P(('dp', 'fsdp')), may hold values from -0.1875 to 0.1875
- b_query: bfloat16 [1024], P(('dp', 'fsdp')), may hold values from -1.5 to 1.5
- b_value: bfloat16 [1024], P(('dp', 'fsdp')), may hold values from -1.5 to 1.5
- w_out: bfloat16 [1024, 1024], P(('dp', 'fsdp')), may hold values from -0.75 to 0.75
- b_out: bfloat16 [1024], P(('dp', 'fsdp')), may hold values from -1.5 to 1.5
- gain_one: bfloat16 [1024], P(('dp', 'fsdp')), may hold values from 0.099609375 to 1.8984375
- shift_one: bfloat16 [1024], P(('dp', 'fsdp')), may hold values from -1.5 to 1.5
- w_in: bfloat16 [1024, 4096], P(('dp', 'fsdp')), may hold values from -0.1875 to 0.1875
- b_in: bfloat16 [4096], P(('dp', 'fsdp')), may hold values from -1.5 to 1.5
- w_back: bfloat16 [4096, 1024], P(('dp', 'fsdp')), may hold values from -0.09375 to 0.09375
- b_back: bfloat16 [1024], P(('dp', 'fsdp')), may hold values from -1.5 to 1.5
- gain_two: bfloat16 [1024], P(('dp', 'fsdp')), may hold values from 0.099609375 to 1.8984375
- shift_two: bfloat16 [1024], P(('dp', 'fsdp')), may hold values from -1.5 to 1.5
- cotangent: bfloat16 [8192, 1024], P(('dp', 'fsdp')), may hold values from -6 to 6
Outputs:
- layer_out: bfloat16 [8192, 1024], P(('dp', 'fsdp'))
- grad_tokens: float32 [8192, 1024], P(('dp', 'fsdp'))
- grad_w_qkv: float32 [1024, 3072], P(('dp', 'fsdp'))
- grad_b_query: float32 [1024], P(('dp', 'fsdp'))
- grad_b_value: float32 [1024], P(('dp', 'fsdp'))
- grad_w_out: float32 [1024, 1024], P(('dp', 'fsdp'))
- grad_b_out: float32 [1024], P(('dp', 'fsdp'))
- grad_gain_one: float32 [1024], P(('dp', 'fsdp'))
- grad_shift_one: float32 [1024], P(('dp', 'fsdp'))
- grad_w_in: float32 [1024, 4096], P(('dp', 'fsdp'))
- grad_b_in: float32 [4096], P(('dp', 'fsdp'))
- grad_w_back: float32 [4096, 1024], P(('dp', 'fsdp'))
- grad_b_back: float32 [1024], P(('dp', 'fsdp'))
- grad_gain_two: float32 [1024], P(('dp', 'fsdp'))
- grad_shift_two: float32 [1024], P(('dp', 'fsdp'))
- root_squares: float32 [3], replicated
The draws below stay inside these ranges and needn't reach their ends.
Inputs may be any that keep to these rules, and one draw needn't show every extreme that they name: `segments`: within each sequence segment numbers never fall, start at 0 (padding, at least one token) and take every value to 7; every segment has 1 to 64 tokens and one has exactly 64.
All inputs are finite; a program needn't handle non-finite values.
Results may differ from the reference program's by a relative error of at most 0.013.
Values may be sent and summed in bfloat16 or wider, within the bound.
No kernel may reach another device: no remote copies, remote signals or barrier semaphores. Data moves between devices by JAX's collectives and lax.ppermute only.
A program may use at most 192 MiB of HBM per device.

```python
import math
import jax
import jax.numpy as jnp
import numpy as np
from jax import lax

D = 1024
HEADS = 16
HEAD_DIM = 64
FF = 4096
SEQ = 128
SEGS = 8
DOC_MOST = 64
SEQS = 64
TOKENS = 8192


def draw_tokens(key, part):
    rising = 1.0 + 0.7 * jnp.arange(TOKENS, dtype=jnp.float32) / max(TOKENS - 1, 1)
    noise = jax.random.truncated_normal(key, -4.0, 4.0, (TOKENS, D), jnp.float32)
    return (noise * rising[:, None]).astype(jnp.bfloat16)


def block_scale(rng, extent, split, smallest, top_value):
    loudness, own = 1.0, jax.random.fold_in(rng, 6)
    for axis_at, shards_of in split:
        heights = jnp.exp(jax.random.uniform(jax.random.fold_in(own, axis_at), (shards_of,), jnp.float32, smallest / len(split), top_value / len(split)))
        loudness = loudness * jnp.repeat(heights, extent[axis_at] // shards_of).reshape([-1 if axis == axis_at else 1 for axis in range(len(extent))])
    return loudness


def split_up(count, total, limit, skew):
    portions = [(1 << 20) // math.isqrt(standing ** skew) + 1 for standing in range(2, count + 1)]
    rest, holding = total - limit - (count - 1), [1] * (count - 1)
    while rest > 0:
        candidates = [i for i in range(count - 1) if holding[i] < limit]
        mass, remaining = sum([portions[i] for i in candidates]), rest
        for i in candidates:
            addition = min(limit - holding[i], max(1, remaining * portions[i] // mass), rest)
            holding[i] = holding[i] + addition
            rest = rest - addition
    return np.array([limit] + holding)


def ragged(rng, count, total, bound, lean):
    if count == 2:
        one = jax.random.randint(rng, (), max(1, total - bound), min(bound, total - 1) + 1)
        return jnp.stack([one, total - one])
    sizes = jnp.asarray(split_up(count, total, bound, lean), jnp.int32)
    pairs = (count - 1) // 2
    giver, sink = sizes[1:1 + 2 * pairs:2], sizes[2:2 + 2 * pairs:2]
    slack = jnp.minimum(giver - 1, bound - sink)
    shifted = jax.random.randint(jax.random.fold_in(rng, 1), (pairs,), 0, 1 << 20) % (slack + 1)
    sizes = sizes.at[1:1 + 2 * pairs:2].set(giver - shifted).at[2:2 + 2 * pairs:2].set(sink + shifted)
    return sizes[jax.random.permutation(jax.random.fold_in(rng, 2), count)]


def scatter_about(rng, extent, spread, reach, pieces=(), held_as=jnp.bfloat16):
    drawn = jax.random.normal(rng, extent, jnp.float32) * spread
    if len(pieces) > 0:
        drawn = block_scale(rng, extent, pieces, -0.22, 0.18) * drawn
    return jnp.clip(drawn, min=-reach, max=reach).astype(held_as)


def setup_inputs(seed: int = 0) -> dict:
    streams_of = jax.random.split(jax.random.key(seed), 17)
    tokens = draw_tokens(jax.random.fold_in(streams_of[16], 71), 0)
    segments = jax.vmap(lambda own: jnp.searchsorted(jnp.cumsum(ragged(own, SEGS, SEQ, DOC_MOST, 2)), jnp.arange(SEQ), side="right"))(jax.random.split(streams_of[1], SEQS)).reshape((SEQS, SEQ)).astype(jnp.int32)
    w_qkv = scatter_about(streams_of[2], (D, 3 * D), D ** -0.5, 0.1875, ((0, 32),))
    b_query = scatter_about(streams_of[3], (D,), 0.3, 1.5, ((0, 32),))
    b_value = scatter_about(streams_of[4], (D,), 0.3, 1.5, ((0, 32),))
    w_out = scatter_about(streams_of[5], (D, D), (D // 16) ** -0.5, 0.75, ((0, 32),))
    b_out = scatter_about(streams_of[6], (D,), 0.3, 1.5, ((0, 32),))
    gain_one = jnp.clip(1.0 + 0.18 * jax.random.normal(streams_of[7], (D,), jnp.float32), 0.099609375, 1.8984375).astype(jnp.bfloat16)
    shift_one = scatter_about(streams_of[8], (D,), 0.3, 1.5, ((0, 32),))
    w_in = scatter_about(streams_of[9], (D, FF), D ** -0.5, 0.1875, ((0, 32),))
    b_in = scatter_about(streams_of[10], (FF,), 0.3, 1.5, ((0, 32),))
    w_back = scatter_about(streams_of[11], (FF, D), FF ** -0.5, 0.09375, ((0, 32),))
    b_back = scatter_about(streams_of[12], (D,), 0.3, 1.5, ((0, 32),))
    gain_two = jnp.clip(1.0 + 0.18 * jax.random.normal(streams_of[13], (D,), jnp.float32), 0.099609375, 1.8984375).astype(jnp.bfloat16)
    shift_two = scatter_about(streams_of[14], (D,), 0.3, 1.5, ((0, 32),))
    cotangent = scatter_about(streams_of[15], (TOKENS, D), 1.0, 6.0, ((0, 32),))
    return {"tokens": tokens, "segments": segments, "w_qkv": w_qkv, "b_query": b_query, "b_value": b_value, "w_out": w_out, "b_out": b_out, "gain_one": gain_one, "shift_one": shift_one, "w_in": w_in, "b_in": b_in, "w_back": w_back, "b_back": b_back, "gain_two": gain_two, "shift_two": shift_two, "cotangent": cotangent}


@jax.custom_vjp
def low(v):
    return lax.optimization_barrier(v.astype(jnp.bfloat16)).astype(jnp.float32)

@jax.custom_vjp
def low_back(v):
    return v

def low_keep(v):
    return (low(v), None)

def low_pass(kept, grad):
    return (grad,)

def back_keep(v):
    return (v, None)

def back_low(kept, grad):
    return (low(grad),)
low.defvjp(low_keep, low_pass)
low_back.defvjp(back_keep, back_low)

def product(left, right):
    return jnp.dot(left, right, precision=lax.Precision.HIGHEST, preferred_element_type=jnp.float32)

def layer_norm(value, gain, shift):
    centre = lax.optimization_barrier(jnp.mean(value, -1, keepdims=True))
    centred = value - centre
    variance = lax.optimization_barrier(jnp.mean(centred * centred, -1, keepdims=True))
    return centred * lax.rsqrt(variance + 1e-05) * gain + shift

def layer_seq(token_rows, segment_ids, weights):
    w_qkv, b_query, b_value, w_out, b_out, gain_one, shift_one, w_in, b_in, w_back, b_back, gain_two, shift_two = weights
    qkv_bias = jnp.concatenate([b_query, jnp.zeros_like(b_query), b_value])
    qkv = low(low_back(product(token_rows, w_qkv) + qkv_bias))
    split_heads = qkv.reshape(SEQ, 3, HEADS, HEAD_DIM)
    query_heads = split_heads[:, 0]
    key_heads = split_heads[:, 1]
    value_heads = split_heads[:, 2]
    score_scale = HEAD_DIM ** (-0.5)
    scores = low_back(jnp.einsum('qhd,khd->hqk', query_heads, key_heads, precision=lax.Precision.HIGHEST) * score_scale)
    same_doc = segment_ids[:, None] == segment_ids[None, :]
    masked = jnp.where(same_doc[None], scores, -1e+30)
    attention_probs = low(jax.nn.softmax(masked, axis=-1))
    attn = jnp.einsum('hqk,khd->qhd', attention_probs, value_heads, precision=lax.Precision.HIGHEST)
    attn = low(low_back(attn.reshape(SEQ, D)))
    branch = low_back(product(attn, w_out) + b_out)
    residual_mid = token_rows + branch
    normed_one = layer_norm(residual_mid, gain_one, shift_one)
    normed_low = low(normed_one)
    hidden = low_back(product(normed_low, w_in) + b_in)
    activation = low(jax.nn.gelu(hidden, approximate=False))
    mlp_out = low_back(product(activation, w_back) + b_back)
    normed_out = layer_norm(normed_one + mlp_out, gain_two, shift_two)
    valid_rows = (segment_ids > 0).astype(jnp.float32)[:, None]
    partial_value = jnp.stack([jnp.sum(valid_rows * token_rows * token_rows), jnp.sum(valid_rows * branch * branch), jnp.sum(valid_rows * residual_mid * residual_mid), jnp.sum(valid_rows)])
    return (normed_out, partial_value)

def reference(tokens, segments, w_qkv, b_query, b_value, w_out, b_out, gain_one, shift_one, w_in, b_in, w_back, b_back, gain_two, shift_two, cotangent):
    weights = tuple((item.astype(jnp.float32) for item in (w_qkv, b_query, b_value, w_out, b_out, gain_one, shift_one, w_in, b_in, w_back, b_back, gain_two, shift_two)))
    inputs = tokens.astype(jnp.float32).reshape(SEQS, SEQ, D)

    def whole(inputs, weights):

        def step(carry, item):
            token_rows, segment_ids = item
            normed, partial_value = jax.checkpoint(layer_seq)(token_rows, segment_ids, weights)
            return (carry, (normed, partial_value))
        carry, (normed, partial_value) = lax.scan(step, jnp.zeros((), jnp.float32), (inputs, segments))
        return (normed, partial_value)
    normed, pull_back, partial_value = jax.vjp(whole, inputs, weights, has_aux=True)
    grad_inputs, grad_weights = pull_back(cotangent.astype(jnp.float32).reshape(SEQS, SEQ, D))
    totals = lax.optimization_barrier(jnp.sum(partial_value, 0))
    root_squares = jnp.sqrt(totals[:3] / (totals[3] * D))
    return (normed.reshape(TOKENS, D).astype(jnp.bfloat16), grad_inputs.reshape(TOKENS, D), grad_weights[0], grad_weights[1], grad_weights[2], grad_weights[3], grad_weights[4], grad_weights[5], grad_weights[6], grad_weights[7], grad_weights[8], grad_weights[9], grad_weights[10], grad_weights[11], grad_weights[12], root_squares)
```

```python
import jax
import jax.numpy as jnp
from jax import lax
from jax.experimental import pallas as pl
from jax.experimental.pallas import tpu as pltpu
from jax.sharding import PartitionSpec as P

HEADS = 16
BF = jnp.bfloat16
F32 = jnp.float32
MOST_DIRECT = 8


def dot(a, b, ca=1, cb=0):
    return lax.dot_general(a, b, (((ca,), (cb,)), ((), ())), preferred_element_type=F32)


def swap(value, bit):
    size = lax.axis_size("fsdp")
    return lax.ppermute(value, "fsdp", [(i, i ^ bit) for i in range(size)])


def group_gather(value):
    two = jnp.concatenate([value, swap(value, 2)], 0)
    return jnp.concatenate([two, swap(two, 1)], 0)


def group_reduce(part, axis=0):
    half = part.shape[axis] // 2
    quarter = half // 2
    take = lambda v, a, n: lax.slice_in_dim(v, a, a + n, axis=axis)
    got = swap(take(part, half, half).astype(BF), 1)
    far = take(part, quarter, quarter) + take(got, quarter, quarter).astype(F32)
    got_far = swap(far.astype(BF), 2)
    return take(part, 0, quarter) + take(got, 0, quarter).astype(F32) + got_far.astype(F32)


def flip_blocks(value, me, axis):
    size = value.shape[axis] // 4
    parts = [lax.slice_in_dim(value, i * size, (i + 1) * size, axis=axis) for i in range(4)]
    low = me % 2 == 0
    parts = [jnp.where(low, parts[i], parts[i ^ 1]) for i in range(4)]
    high = me // 2 == 0
    parts = [jnp.where(high, parts[i], parts[i ^ 2]) for i in range(4)]
    return jnp.concatenate(parts, axis)


def swap_middle(value, axis):
    size = value.shape[axis] // 4
    parts = [lax.slice_in_dim(value, i * size, (i + 1) * size, axis=axis) for i in (0, 2, 1, 3)]
    return jnp.concatenate(parts, axis)


def to_group(value, me, axis):
    return swap_middle(flip_blocks(value, me, axis), axis)


def from_group(value, me, axis):
    return flip_blocks(swap_middle(value, axis), me, axis)


def scatter_columns(blocks, me):
    far, near = me // 2, me % 2
    pairs = blocks.reshape(2, 2, *blocks.shape[1:])
    keep = lax.dynamic_index_in_dim(pairs, far, 0, keepdims=False)
    got = swap(lax.dynamic_index_in_dim(pairs, 1 - far, 0, keepdims=False), 2)
    both = jnp.stack([keep, got])
    mine = lax.dynamic_index_in_dim(both, near, 1, keepdims=False)
    other = swap(lax.dynamic_index_in_dim(both, 1 - near, 1, keepdims=False), 1)
    four = jnp.concatenate([mine, other], 0)
    a, b, c, d = four[0], four[1], four[2], four[3]
    here = near == 0
    even, odd = (jnp.where(here, a, c), jnp.where(here, b, d)), (
        jnp.where(here, c, a),
        jnp.where(here, d, b),
    )
    first = far == 0
    rows = [
        jnp.where(first, even[0], even[1]),
        jnp.where(first, odd[0], odd[1]),
        jnp.where(first, even[1], even[0]),
        jnp.where(first, odd[1], odd[0]),
    ]
    return rows


def data_shape():
    size = lax.axis_size("dp")
    return size // 2, 2


def data_swap(value):
    size = lax.axis_size("dp")
    return lax.ppermute(value, "dp", [(i, i ^ 1) for i in range(size)])


def data_from(value, offset):
    high, low = data_shape()
    pairs = [(h * low + b, ((h - offset) % high) * low + b) for h in range(high) for b in range(low)]
    return lax.ppermute(value, "dp", pairs)


def data_gather(value):
    high, low = data_shape()
    if high <= MOST_DIRECT:
        own = jnp.concatenate([value] + [data_from(value, k) for k in range(1, high)], 0)
        return own, data_swap(own)
    me = lax.axis_index("dp")
    whole = lax.all_gather(value, "dp", axis=0).reshape(high, low, *value.shape)
    whole = jnp.roll(whole, (-(me // low), -(me % low)), (0, 1))
    flat = lambda v: v.reshape(high * value.shape[0], *value.shape[1:])
    return flat(whole[:, 0]), flat(whole[:, 1])


def data_reduce(own, other):
    high, low = data_shape()
    rows = own.shape[0] // high
    if high <= MOST_DIRECT:
        summed = own.astype(F32) + data_swap(other).astype(F32)
        total = summed[:rows]
        low_sum = summed.astype(other.dtype)
        for k in range(1, high):
            total = total + data_from(low_sum[k * rows : (k + 1) * rows], high - k).astype(F32)
        return total
    me = lax.axis_index("dp")
    both = jnp.stack([v.reshape(high, rows, *v.shape[1:]) for v in (own, other)], 1)
    both = jnp.roll(both.astype(other.dtype), (me // low, me % low), (0, 1))
    flat = both.reshape(high * low * rows, *own.shape[1:])
    return lax.psum_scatter(flat, "dp", scatter_dimension=0, tiled=True).astype(F32)


def data_columns(value, back=False):
    high, low = data_shape()
    me = lax.axis_index("dp")
    h, b = me // low, me % low
    width = value.shape[1] // (high * low)
    parts = []
    if back:
        for k in range(high):
            for j in range(low):
                at = ((j - b) % low) * high + (k - h) % high
                parts.append(lax.dynamic_slice_in_dim(value, at * width, width, 1))
    else:
        for j in range(low):
            for k in range(high):
                at = ((h + k) % high) * low + (b + j) % low
                parts.append(lax.dynamic_slice_in_dim(value, at * width, width, 1))
    return jnp.concatenate(parts, 1)


def attend(q_ref, seg_row, seg_col, out_ref):
    width = out_ref.shape[1]
    same = seg_col[0] == seg_row[0]
    for h in range(width // 64):
        at = h * 64
        q = q_ref[:, at : at + 64]
        k = q_ref[:, width + at : width + at + 64]
        v = q_ref[:, 2 * width + at : 2 * width + at + 64]
        scores = dot(q, k, 1, 1) * (64**-0.5)
        masked = jnp.where(same, scores, -1e30)
        exponent = jnp.exp(masked - jnp.max(masked, -1, keepdims=True))
        probs = exponent / jnp.sum(exponent, -1, keepdims=True)
        out_ref[:, at : at + 64] = dot(probs.astype(BF), v).astype(BF)


def attend_back(q_ref, d_ref, seg_row, seg_col, out_ref):
    width = d_ref.shape[1]
    same = seg_col[0] == seg_row[0]
    for h in range(width // 64):
        at = h * 64
        q = q_ref[:, at : at + 64]
        k = q_ref[:, width + at : width + at + 64]
        v = q_ref[:, 2 * width + at : 2 * width + at + 64]
        d = d_ref[:, at : at + 64]
        scores = dot(q, k, 1, 1) * (64**-0.5)
        masked = jnp.where(same, scores, -1e30)
        exponent = jnp.exp(masked - jnp.max(masked, -1, keepdims=True))
        probs = exponent / jnp.sum(exponent, -1, keepdims=True)
        d_probs = dot(d, v, 1, 1)
        d_scores = probs * (d_probs - jnp.sum(d_probs * probs, -1, keepdims=True))
        d_scores = d_scores.astype(BF)
        out_ref[:, at : at + 64] = (dot(d_scores, k) * (64**-0.5)).astype(BF)
        out_ref[:, width + at : width + at + 64] = (dot(d_scores, q, 0, 0) * (64**-0.5)).astype(BF)
        out_ref[:, 2 * width + at : 2 * width + at + 64] = dot(probs.astype(BF), d, 0, 0).astype(BF)


def attention(qkv, seg):
    count, length = seg.shape
    width = qkv.shape[1] // 3
    return pl.pallas_call(
        attend,
        grid=(count,),
        in_specs=[
            pl.BlockSpec((length, 3 * width), lambda i: (i, 0)),
            pl.BlockSpec((1, 1, length), lambda i: (i, 0, 0)),
            pl.BlockSpec((1, length, 1), lambda i: (i, 0, 0)),
        ],
        out_specs=pl.BlockSpec((length, width), lambda i: (i, 0)),
        out_shape=jax.ShapeDtypeStruct((qkv.shape[0], width), BF),
        name="attend",
    )(qkv, seg[:, None, :], seg[:, :, None])


def attention_back(qkv, d_attn, seg):
    count, length = seg.shape
    width = d_attn.shape[1]
    return pl.pallas_call(
        attend_back,
        grid=(count,),
        in_specs=[
            pl.BlockSpec((length, 3 * width), lambda i: (i, 0)),
            pl.BlockSpec((length, width), lambda i: (i, 0)),
            pl.BlockSpec((1, 1, length), lambda i: (i, 0, 0)),
            pl.BlockSpec((1, length, 1), lambda i: (i, 0, 0)),
        ],
        out_specs=pl.BlockSpec((length, 3 * width), lambda i: (i, 0)),
        out_shape=jax.ShapeDtypeStruct((qkv.shape[0], 3 * width), BF),
        name="attend_back",
    )(qkv, d_attn, seg[:, None, :], seg[:, :, None])


def norm_parts(value):
    centred = value - jnp.mean(value, -1, keepdims=True)
    inverse = lax.rsqrt(jnp.mean(centred * centred, -1, keepdims=True) + 1e-05)
    return centred * inverse, inverse


def norm_back(grad, unit, inverse, gain):
    scaled = grad * gain
    mean = jnp.mean(scaled, -1, keepdims=True)
    along = jnp.mean(scaled * unit, -1, keepdims=True)
    return (scaled - mean - unit * along) * inverse, jnp.sum(grad * unit, 0), jnp.sum(grad, 0)


def per_device(
    tokens,
    segments,
    w_qkv,
    b_query,
    b_value,
    w_out,
    b_out,
    gain_one,
    shift_one,
    w_in,
    b_in,
    w_back,
    b_back,
    gain_two,
    shift_two,
    cotangent,
):
    data_size, group_size = lax.axis_size("dp"), lax.axis_size("fsdp")
    me, place = lax.axis_index("fsdp"), lax.axis_index("dp")
    high, low = data_shape()
    mine, model = tokens.shape
    rows = w_qkv.shape[0]
    width = model // group_size
    hidden_rows = w_back.shape[0]
    half = model // low

    def cut(weight, parts):
        return weight.reshape(rows, parts, group_size, -1)

    qkv_cut = cut(w_qkv, 3)
    out_cut = cut(w_out, 1)
    qo_send = jnp.stack(
        [
            jnp.concatenate([qkv_cut[:, 0, i], qkv_cut[:, 1, i], qkv_cut[:, 2, i], out_cut[:, 0, i]], 1)
            for i in range(group_size)
        ]
    )
    in_cut = w_in.reshape(rows, data_size, group_size, hidden_rows)
    in_send = jnp.stack([in_cut[:, :, i].reshape(rows, -1) for i in range(group_size)])
    qo_shard = jnp.concatenate(scatter_columns(qo_send, me), 0)
    x_rel = data_columns(tokens)
    x_all = group_gather(x_rel)
    seg_all = group_gather(segments)
    qo_a, qo_b = data_gather(qo_shard)

    vectors = (b_query, b_value, b_out, gain_one, shift_one, b_back, gain_two, shift_two)
    pack = jnp.concatenate(vectors + (b_in,))
    count = len(vectors)
    pack_length = pack.shape[0]
    room = -(-pack_length // 128) * 128
    pack = jnp.pad(pack, (0, room - pack_length))[None]
    pack = from_group(group_gather(pack), me, 0).reshape(1, group_size * room)
    pack_a, pack_b = data_gather(pack)
    pack_all = jnp.stack([pack_a, pack_b], 1)
    pack_all = jnp.roll(pack_all, (place // low, place % low), (0, 1))
    pack_all = pack_all.reshape(data_size, group_size, room)
    by_vector = pack_all[:, :, : count * rows].reshape(data_size, group_size, count, rows)
    by_vector = by_vector.transpose(2, 0, 1, 3).reshape(count, model).astype(F32)
    v_query, v_value, v_out, v_gain_one, v_shift_one, v_back, v_gain_two, v_shift_two = by_vector
    v_in = lax.dynamic_index_in_dim(pack_all, me, 1, keepdims=False)
    v_in = v_in[:, count * rows : pack_length].reshape(1, -1).astype(F32)
    v_in = data_columns(v_in)

    in_shard = jnp.concatenate(scatter_columns(in_send, me), 0)
    in_a, in_b = data_gather(in_shard)
    back_a, back_b = data_gather(w_back)

    q_bias = lax.dynamic_slice_in_dim(v_query, me * width, width)
    v_bias = lax.dynamic_slice_in_dim(v_value, me * width, width)
    qkv_bias = jnp.concatenate([q_bias, jnp.zeros_like(q_bias), v_bias])
    w_qkv_a, w_qkv_b = qo_a[:, : 3 * width], qo_b[:, : 3 * width]
    x_a, x_b = x_all[:, :half], x_all[:, half:]
    qkv = (dot(x_a, w_qkv_a) + dot(x_b, w_qkv_b) + qkv_bias).astype(BF)
    attn_heads = attention(qkv, seg_all)
    two = 2 * mine
    other = swap(attn_heads[two:], 1)
    pair = jnp.concatenate([attn_heads[:two], other], 1)
    attn = jnp.concatenate([pair[:mine], swap(pair[mine:], 2)], 1)
    attn = data_columns(flip_blocks(attn, me, 1))

    out_cols = jnp.concatenate([qo_a[:, 3 * width :], qo_b[:, 3 * width :]], 0)
    out_two = jnp.concatenate([out_cols, swap(out_cols, 2)], 1)
    out_all = jnp.concatenate([out_two, swap(out_two, 1)], 1)
    branch = from_group(dot(attn, out_all), me, 1) + v_out
    token_float = tokens.astype(F32)
    mid = token_float + branch
    unit_one, inverse_one = norm_parts(mid)
    y_one = unit_one * v_gain_one + v_shift_one
    y_rel = data_columns(y_one.astype(BF))
    y_all = group_gather(y_rel)

    valid = (segments > 0).astype(F32).reshape(mine, 1)
    stats = jnp.stack(
        [
            jnp.sum(valid * token_float * token_float),
            jnp.sum(valid * branch * branch),
            jnp.sum(valid * mid * mid),
            jnp.sum(valid),
        ]
    )

    in_a, in_b = data_columns(in_a), data_columns(in_b)
    y_a, y_b = y_all[:, :half], y_all[:, half:]
    hidden = dot(y_a, in_a) + dot(y_b, in_b) + v_in
    below = 0.5 * (1.0 + lax.erf(hidden * (2.0**-0.5)))
    activation = (hidden * below).astype(BF)
    hidden_half = activation.shape[1] // low
    act_a, act_b = activation[:, :hidden_half], activation[:, hidden_half:]
    slope = below + hidden * jnp.exp(-0.5 * hidden * hidden) * 0.3989422804014327
    mlp_part = dot(act_a, back_a) + dot(act_b, back_b)
    mlp_out = group_reduce(mlp_part) + v_back
    summed = y_one + mlp_out
    unit_two, inverse_two = norm_parts(summed)
    layer_out = (unit_two * v_gain_two + v_shift_two).astype(BF)

    cot = cotangent.astype(F32)
    d_summed, g_gain_two, g_shift_two = norm_back(cot, unit_two, inverse_two, v_gain_two)
    d_mlp = d_summed.astype(BF)
    g_b_back = jnp.sum(d_mlp.astype(F32), 0)
    d_all = group_gather(d_mlp)
    g_back_b = dot(act_b, d_all, 0, 0).astype(BF)
    g_back_a = dot(act_a, d_all, 0, 0).astype(BF)
    grad_w_back = data_reduce(g_back_a, g_back_b)
    d_act = jnp.concatenate([dot(d_all, back_a, 1, 1), dot(d_all, back_b, 1, 1)], 1)
    d_hidden = (d_act * slope).astype(BF)
    g_b_in = jnp.sum(d_hidden.astype(F32), 0)
    d_y_part = jnp.concatenate([dot(d_hidden, in_a, 1, 1), dot(d_hidden, in_b, 1, 1)], 1)
    d_hidden_whole = data_columns(d_hidden, back=True)
    g_in_b = dot(y_b, d_hidden_whole, 0, 0).astype(BF)
    g_in_a = dot(y_a, d_hidden_whole, 0, 0).astype(BF)
    g_in = data_reduce(g_in_a, g_in_b)
    d_normed = d_summed + data_columns(group_reduce(d_y_part), back=True)
    d_mid, g_gain_one, g_shift_one = norm_back(d_normed, unit_one, inverse_one, v_gain_one)
    d_branch = d_mid.astype(BF)
    g_b_out = jnp.sum(d_branch.astype(F32), 0)
    d_branch_x = to_group(d_branch, me, 1)
    d_attn = dot(d_branch_x, out_all, 1, 1).astype(BF)
    d_attn = flip_blocks(data_columns(d_attn, back=True), me, 1)
    near_heads, far_heads = d_attn[:, : 2 * width], d_attn[:, 2 * width :]
    d_pair = jnp.concatenate([near_heads, swap(far_heads, 2)], 0)
    d_heads = jnp.concatenate([d_pair[:, :width], swap(d_pair[:, width:], 1)], 0)
    g_out = group_reduce(dot(attn, d_branch_x, 0, 0), 1)
    d_qkv = attention_back(qkv, d_heads, seg_all)
    g_qkv_bias = jnp.sum(d_qkv.astype(F32), 0)
    g_out = g_out.astype(BF)
    g_qo_b = jnp.concatenate([dot(x_b, d_qkv, 0, 0).astype(BF), g_out[half:]], 1)
    g_qo_a = jnp.concatenate([dot(x_a, d_qkv, 0, 0).astype(BF), g_out[:half]], 1)
    g_qo = data_reduce(g_qo_a, g_qo_b)
    d_x_part = jnp.concatenate([dot(d_qkv, w_qkv_a, 1, 1), dot(d_qkv, w_qkv_b, 1, 1)], 1)
    grad_tokens = d_mid + data_columns(group_reduce(d_x_part), back=True)

    g_qo = scatter_columns(g_qo.astype(BF).reshape(group_size, rows, -1), me)
    g_in = scatter_columns(g_in.astype(BF).reshape(group_size, rows, -1), me)
    grad_w_qkv = jnp.concatenate(
        [g_qo[f][:, p * width : (p + 1) * width] for p in range(3) for f in range(group_size)], 1
    ).astype(F32)
    grad_w_out = jnp.concatenate([g[:, 3 * width :] for g in g_qo], 1).astype(F32)
    grad_w_in = jnp.stack(
        [g.reshape(rows, data_size, hidden_rows) for g in g_in], 2
    ).reshape(rows, -1).astype(F32)

    spread = lambda v: lax.dynamic_update_slice_in_dim(jnp.zeros((model,), F32), v, me * width, 0)
    small = jnp.stack(
        [
            spread(g_qkv_bias[:width]),
            spread(g_qkv_bias[2 * width :]),
            g_b_out,
            g_gain_one,
            g_shift_one,
            g_b_back,
            g_gain_two,
            g_shift_two,
        ]
    )
    small = small.reshape(count, data_size, group_size, rows).transpose(1, 2, 0, 3)
    small = small.reshape(data_size, group_size, count * rows)
    in_bias = data_columns(g_b_in[None], back=True).reshape(data_size, 1, hidden_rows)
    in_bias = jnp.where(jnp.arange(group_size)[None, :, None] == me, in_bias, 0.0)
    spare = -(-(pack_length + 4) // 128) * 128 - pack_length - 4
    small = jnp.concatenate(
        [
            small,
            in_bias,
            jnp.broadcast_to(stats, (data_size, group_size, 4)),
            jnp.zeros((data_size, group_size, spare), F32),
        ],
        2,
    )
    length = small.shape[2]
    small = flip_blocks(small, me, 1).reshape(data_size, 2, 2, length)
    small = small.transpose(2, 1, 0, 3)
    small = small[0] + swap(small[1], 1)
    small = small[0] + swap(small[1], 2)
    small = small.reshape(high, low, length)
    small = jnp.roll(small, (-(place // low), -(place % low)), (0, 1))
    small = data_reduce(small[:, 0], small[:, 1])[0]
    grads = [small[i * rows : (i + 1) * rows] for i in range(count)]
    g_query, g_value, g_out_bias, g_g1, g_s1, g_back_bias, g_g2, g_s2 = grads
    grad_b_in = small[count * rows : pack_length]
    totals = small[pack_length : pack_length + 4]
    root_squares = jnp.sqrt(totals[:3] / (totals[3] * model))
    return (
        layer_out,
        grad_tokens,
        grad_w_qkv,
        g_query,
        g_value,
        grad_w_out,
        g_out_bias,
        g_g1,
        g_s1,
        grad_w_in,
        grad_b_in,
        grad_w_back,
        g_back_bias,
        g_g2,
        g_s2,
        root_squares,
    )


def solution(mesh):
    rows, flat = P(("dp", "fsdp"), None), P(("dp", "fsdp"))
    return jax.shard_map(
        per_device,
        mesh=mesh,
        in_specs=(
            rows,
            rows,
            rows,
            flat,
            flat,
            rows,
            flat,
            flat,
            flat,
            rows,
            flat,
            rows,
            flat,
            flat,
            flat,
            rows,
        ),
        out_specs=(
            rows,
            rows,
            rows,
            flat,
            flat,
            rows,
            flat,
            flat,
            flat,
            rows,
            flat,
            rows,
            flat,
            flat,
            flat,
            P(),
        ),
        check_vma=False,
    )
```
